32 devices in a mesh: gz: 8 (over z, x), gy: 4 (over y, core).
Axes of the slice: x: 2, y: 2, z: 4, core: 2. Of those that a mesh axis runs over, the one named last changes fastest.
Arguments:
- parcel_cell: int32 [131072], P(('gz', 'gy')), may hold values from 0 to 131071
- parcel_offset: float32 [3, 131072], P(None, ('gz', 'gy')), may hold values from 0 to 1
- parcel_volume: float32 [131072], P(('gz', 'gy')), may hold values from 1 to 8
- parcel_force: float32 [3, 131072], P(None, ('gz', 'gy')), may hold values from -24 to 24
- brick_counts: int32 [8, 4], P('gz', 'gy'), may hold values from 1 to 4096, as said below
- divergence: float32 [64, 256, 256], P('gz', 'gy'), may hold values from -6 to 6
- pressure_prev: float32 [64, 256, 256], P('gz', 'gy'), may hold values from -6 to 6
- gas_density: float32 [64, 256, 256], P('gz', 'gy'), may hold values from 0.5 to 2
Outputs:
- gas_fraction: float32 [64, 256, 256], P('gz', 'gy')
- momentum_source: float32 [64, 3, 256, 256], P('gz', None, 'gy')
- pressure: float32 [64, 256, 256], P('gz', 'gy')
- residual: float32 [64, 256, 256], P('gz', 'gy')
The draws below stay inside these ranges and needn't reach their ends.
Inputs may be any that keep to these rules, and one draw needn't show every extreme that they name: brick_counts gives the number of live parcels of each brick, held in the brick's first slots; one brick holds exactly 4096 and one exactly 1.
All inputs are finite; a program needn't handle non-finite values.
Results may differ from the reference program's by a relative error of at most 0.0021.
Values sent between devices are 32-bit elements; how exact they have to be, the bound alone decides.
A program may use at most 64 MiB of HBM per device.

```python
import math
import jax
import jax.numpy as jnp
from jax import lax

CZ = 8
CY = 64
CX = 256
PCAP = 4096
SWEEPS = 3
ITERS = 2
BRICKS_Z = 8
BRICKS_Y = 4
NZ = 64
NY = 256
NX = 256
PARCELS = 131072


def draw_brick_counts(key, part):
    key_level = jax.random.fold_in(key, 11)
    key_jitter = jax.random.fold_in(key, 12)
    key_ranking = jax.random.fold_in(key, 13)
    bricks = BRICKS_Z * BRICKS_Y
    levels = jax.random.randint(key_level, (bricks,), 0, 4)
    jitter = jax.random.randint(key_jitter, (bricks,), 0, 64)
    counts = jnp.maximum(PCAP // jnp.left_shift(1, levels) - jitter, 1)
    ranking = jax.random.permutation(key_ranking, bricks)
    counts = counts.at[ranking[0]].set(PCAP)
    counts = counts.at[ranking[1]].set(1)
    return counts.reshape(BRICKS_Z, BRICKS_Y).astype(jnp.int32)


def plant(values, stream_key, least, high):
    shape = values.shape
    spot = [jax.random.randint(jax.random.fold_in(stream_key, axis), (), 0, shape[axis]) for axis in range(len(shape))]
    values = values.at[tuple(spot)].set(least)
    longest = shape.index(max(shape))
    spot[longest] = (spot[longest] + 1) % shape[longest]
    return values.at[tuple(spot)].set(high)


def steps_of(rng, dims, pieces, low, largest):
    factor_of, own = 1.0, jax.random.fold_in(rng, 6)
    for dim, shards_of in pieces:
        draws = jnp.exp(jax.random.uniform(jax.random.fold_in(own, dim), (shards_of,), jnp.float32, low / len(pieces), largest / len(pieces)))
        factor_of = factor_of * jnp.repeat(draws, dims[dim] // shards_of).reshape([-1 if axis == dim else 1 for axis in range(len(dims))])
    return factor_of


def noise(stream_key, extent, deviation, limit, split=(), kind=jnp.bfloat16):
    values = jax.random.normal(stream_key, extent, jnp.float32) * deviation
    if len(split) > 0:
        values = steps_of(stream_key, extent, split, -0.22, 0.18) * values
    return jnp.clip(values, min=-limit, max=limit).astype(kind)


def setup_inputs(seed: int = 0) -> dict:
    key_list = jax.random.split(jax.random.key(seed), 9)
    parcel_cell = plant(jax.random.randint(key_list[0], (PARCELS,), 0, CZ * CY * CX), jax.random.fold_in(key_list[0], 1), 0, (CZ * CY * CX) - 1).astype(jnp.int32)
    parcel_offset = jnp.clip(1.0 * jax.random.uniform(key_list[1], (3, PARCELS), jnp.float32) ** steps_of(key_list[1], (3, PARCELS), ((1, 32),), -0.2, 0.2), 0.0, 1.0)
    parcel_volume = jnp.clip(jnp.exp(math.log(8.0) - 2.0794415 * jax.random.uniform(key_list[2], (PARCELS,), jnp.float32) ** steps_of(key_list[2], (PARCELS,), ((0, 32),), -0.2, 0.2)), 1.0, 8.0)
    parcel_force = noise(key_list[3], (3, PARCELS), 4.0, 24.0, ((1, 32),), jnp.float32)
    brick_counts = draw_brick_counts(jax.random.fold_in(key_list[8], 71), 0)
    divergence = noise(key_list[5], (NZ, NY, NX), 1.0, 6.0, ((0, 8), (1, 4)), jnp.float32)
    pressure_prev = noise(key_list[6], (NZ, NY, NX), 1.0, 6.0, ((0, 8), (1, 4)), jnp.float32)
    gas_density = jnp.clip(jnp.exp(math.log(2.0) - 1.3862944 * jax.random.uniform(key_list[7], (NZ, NY, NX), jnp.float32) ** steps_of(key_list[7], (NZ, NY, NX), ((0, 8), (1, 4)), -0.2, 0.2)), 0.5, 2.0)
    return dict(parcel_cell=parcel_cell, parcel_offset=parcel_offset, parcel_volume=parcel_volume, parcel_force=parcel_force, brick_counts=brick_counts, divergence=divergence, pressure_prev=pressure_prev, gas_density=gas_density)


smooth_rate = 0.15
stiffness = 0.002


def tap_weight(distance):
    return jnp.exp(-0.5 * distance * distance)


def tap_norm(offset, home_cell, upper_bound):
    summed = jnp.zeros_like(offset)
    for shift_tap in range(-3, 4):
        inside = (home_cell + shift_tap >= 0) & (home_cell + shift_tap < upper_bound)
        summed = summed + jnp.where(inside, tap_weight(shift_tap + 0.5 - offset), 0.0)
    return summed


def axis_weights(home_cell, offset, upper_bound, norm_value):
    tap_list = jnp.arange(-3, 4, dtype=jnp.int32)
    places = home_cell[:, None] + tap_list[None, :]
    distance = tap_list[None, :].astype(jnp.float32) + 0.5 - offset[:, None]
    inside = (places >= 0) & (places < upper_bound)
    weights = jnp.where(inside, tap_weight(distance), 0.0) / norm_value[:, None]
    return weights, jnp.clip(places, 0, upper_bound - 1)


def smooth_field(values):
    size_y, size_x = values.shape[1], values.shape[2]
    padded = jnp.pad(values, ((0, 0), (1, 1), (1, 1)))
    beside = jnp.roll(values, 1, 0) + jnp.roll(values, -1, 0) + padded[:, :-2, 1:-1] + padded[:, 2:, 1:-1] + padded[:, 1:-1, :-2] + padded[:, 1:-1, 2:]
    rows_at = jnp.arange(size_y, dtype=jnp.int32)
    columns = jnp.arange(size_x, dtype=jnp.int32)
    count_y = (rows_at >= 1).astype(jnp.float32) + (rows_at <= size_y - 2).astype(jnp.float32)
    count_x = (columns >= 1).astype(jnp.float32) + (columns <= size_x - 2).astype(jnp.float32)
    neighbour_count = 2.0 + count_y[:, None] + count_x[None, :]
    return values + smooth_rate * (beside - neighbour_count * values)


def neighbour_list(values):
    padded = jnp.pad(values, ((0, 0), (1, 1), (1, 1)))
    return (jnp.roll(values, 1, 0), jnp.roll(values, -1, 0), padded[:, :-2, 1:-1], padded[:, 2:, 1:-1], padded[:, 1:-1, :-2], padded[:, 1:-1, 2:])


def reference(parcel_cell, parcel_offset, parcel_volume, parcel_force, brick_counts, divergence, pressure_prev, gas_density):
    slot_ids = jnp.arange(PARCELS, dtype=jnp.int32)
    brick_ids = slot_ids // PCAP
    live_slots = ((slot_ids - brick_ids * PCAP) < brick_counts.reshape(-1)[brick_ids]).astype(jnp.float32)
    parcel_load = jnp.concatenate([parcel_volume[None, :], parcel_volume[None, :] * parcel_force], axis=0) * live_slots[None, :]
    home_z = (brick_ids // BRICKS_Y) * CZ + parcel_cell // (CY * CX)
    home_y = (brick_ids % BRICKS_Y) * CY + (parcel_cell // CX) % CY
    home_x = parcel_cell % CX
    tap_list = jnp.arange(-3, 4, dtype=jnp.int32)
    norm_z = tap_norm(parcel_offset[0], home_z * 0 + 3, 7)
    distance_z = tap_list[None, :].astype(jnp.float32) + 0.5 - parcel_offset[0][:, None]
    weight_z = tap_weight(distance_z) / norm_z[:, None]
    place_z = (home_z[:, None] + tap_list[None, :]) % NZ
    weight_y, place_y = axis_weights(home_y, parcel_offset[1], NY, tap_norm(parcel_offset[1], home_y, NY))
    weight_x, place_x = axis_weights(home_x, parcel_offset[2], NX, tap_norm(parcel_offset[2], home_x, NX))
    x_weight = lax.optimization_barrier(weight_x.astype(jnp.bfloat16)).astype(jnp.float32)
    component_ids = jnp.arange(4, dtype=jnp.int32)

    def add_plane(deposited, plane_data):
        plane_weight, plane_place = plane_data
        split_weight = (parcel_load * plane_weight[None, :])[:, :, None] * weight_y[None, :, :]
        split_weight = lax.optimization_barrier(split_weight.astype(jnp.bfloat16)).astype(jnp.float32)
        values = split_weight[:, :, :, None] * x_weight[None, :, None, :]
        deposited = deposited.at[plane_place[None, :, None, None], component_ids[:, None, None, None], place_y[None, :, :, None], place_x[None, :, None, :]].add(values)
        return deposited, None

    deposited = jnp.zeros((NZ, 4, NY, NX), jnp.float32)
    deposited, unused_out = lax.scan(add_plane, deposited, (weight_z.T, place_z.T))
    filtered = []
    for component in range(4):
        smoothed = deposited[:, component]
        for sweep_index in range(SWEEPS):
            smoothed = smooth_field(smoothed)
        filtered.append(smoothed)
    gas_fraction = 1.0 / (1.0 + filtered[0])
    momentum_source = jnp.stack(filtered[1:], axis=1)
    mobility = gas_fraction / gas_density
    face_list = [0.5 * (mobility + other) for other in neighbour_list(mobility)]
    diagonal = stiffness * mobility + face_list[0] + face_list[1] + face_list[2] + face_list[3] + face_list[4] + face_list[5]
    along_z = neighbour_list(filtered[1])
    along_y = neighbour_list(filtered[2])
    along_x = neighbour_list(filtered[3])
    spread = 0.5 * (along_z[1] - along_z[0]) + 0.5 * (along_y[3] - along_y[2]) + 0.5 * (along_x[5] - along_x[4])
    right_side = divergence - spread

    def operate(values):
        others = neighbour_list(values)
        coupled = face_list[0] * others[0] + face_list[1] * others[1] + face_list[2] * others[2] + face_list[3] * others[3] + face_list[4] * others[4] + face_list[5] * others[5]
        return diagonal * values - coupled

    pressure = pressure_prev
    residual = right_side - operate(pressure)
    precond = residual / diagonal
    direction = precond
    scaled_norm = jnp.sum(residual * precond)
    for iteration in range(ITERS):
        mapped = operate(direction)
        step_size = scaled_norm / jnp.sum(direction * mapped)
        pressure = pressure + step_size * direction
        residual = residual - step_size * mapped
        if iteration + 1 < ITERS:
            precond = residual / diagonal
            norm_next = jnp.sum(residual * precond)
            direction = precond + (norm_next / scaled_norm) * direction
            scaled_norm = norm_next
    return (gas_fraction, momentum_source, pressure, residual)
```

```python
import functools

import jax
import jax.numpy as jnp
from jax import lax
from jax.experimental import pallas as pl
from jax.experimental.pallas import tpu as pltpu
from jax.sharding import PartitionSpec as P

SWEEPS = 3
REACH = 3
HALO = SWEEPS + 1
EDGE = 2 * HALO
CHUNK = 1024
smooth_rate = 0.15
stiffness = 0.002
F32 = jnp.float32
MESH = pl.DeviceIdType.MESH


def tap(distance):
    return jnp.exp(-0.5 * distance * distance)


def split_cell(cell, ny, nx):
    if ny & (ny - 1) == 0 and nx & (nx - 1) == 0:
        sx, sy = nx.bit_length() - 1, ny.bit_length() - 1
        return (
            lax.shift_right_logical(cell, sx + sy),
            lax.shift_right_logical(cell, sx) & (ny - 1),
            cell & (nx - 1),
        )
    row = lax.div(cell, nx)
    return lax.div(row, ny), lax.rem(row, ny), lax.rem(cell, nx)


def step_kernel(
    ngz, ngy, nz, ny, nx, slots,
    pk_ref, div_ref, p_ref, den_ref,
    gf_ref, mom_ref, out_ref, res_ref,
    near, wz_ref, wy_ref, wx_ref, dep, fld, tile_in,
    halo_z, halo_y, mob, face_z, face_s, face_n, face_w, face_e, diag,
    r_ref, z_ref, q_ref, w_ref, aw_ref, tile_y, tile_z, red_y, red_z,
    near_send, near_recv, tile_send, tile_recv, hz_send, hz_recv, hy_send, hy_recv,
    ry_send, ry_recv, rz_send, rz_recv,
):
    gz, gy = lax.axis_index("gz"), lax.axis_index("gy")
    planes, rows = nz + 2 * HALO, ny + EDGE
    total_y = ngy * ny
    first = gy * ny
    up, down = lax.rem(gz + 1, ngz), lax.rem(gz + ngz - 1, ngz)
    has_s, has_n = gy > 0, gy < ngy - 1

    barrier = pltpu.get_barrier_semaphore()
    for d in range(1, ngz):
        pl.semaphore_signal(barrier, inc=1, device_id={"gz": lax.rem(gz + d, ngz)}, device_id_type=MESH)
    for d in range(1, ngy):
        pl.semaphore_signal(barrier, inc=1, device_id={"gy": lax.rem(gy + d, ngy)}, device_id_type=MESH)
    pl.semaphore_wait(barrier, ngz - 1 + ngy - 1)

    def remote(src, dst, send, recv, where):
        return pltpu.make_async_remote_copy(
            src_ref=src, dst_ref=dst, send_sem=send, recv_sem=recv, device_id=where, device_id_type=MESH
        )

    near_copies = [
        remote(pk_ref, near.at[0], near_send.at[0], near_recv.at[0], {"gz": up}),
        remote(pk_ref, near.at[1], near_send.at[1], near_recv.at[1], {"gz": down}),
    ]
    for c in near_copies:
        c.start()

    def halo_pair(slot, src):
        zc = [
            remote(src.at[nz - 1], halo_z.at[slot, 0], hz_send.at[slot, 0], hz_recv.at[slot, 0], {"gz": up}),
            remote(src.at[0], halo_z.at[slot, 1], hz_send.at[slot, 1], hz_recv.at[slot, 1], {"gz": down}),
        ]
        north = remote(
            src.at[:, pl.ds(ny - 8, 8), :], halo_y.at[slot, 0], hy_send.at[slot, 0], hy_recv.at[slot, 0],
            {"gy": lax.rem(gy + 1, ngy)},
        )
        south = remote(
            src.at[:, pl.ds(0, 8), :], halo_y.at[slot, 1], hy_send.at[slot, 1], hy_recv.at[slot, 1],
            {"gy": lax.rem(gy + ngy - 1, ngy)},
        )
        return zc, north, south

    def halo_start(pair):
        zc, north, south = pair
        for c in zc:
            c.start()

        @pl.when(has_n)
        def _():
            north.start()

        @pl.when(has_s)
        def _():
            south.start()

    def halo_wait(pair):
        zc, north, south = pair
        for c in zc:
            c.wait()

        @pl.when(has_n)
        def _():
            north.wait_send()
            south.wait_recv()

        @pl.when(has_s)
        def _():
            south.wait_send()
            north.wait_recv()

    pair_p, pair_d = halo_pair(0, p_ref), halo_pair(1, den_ref)
    halo_start(pair_d)
    halo_start(pair_p)

    def prepare(pk, brick):
        for at in range(0, slots, CHUNK):
            sl = pl.ds(at, CHUNK)
            cz, cy, cx = split_cell(pk[4:5, sl].astype(jnp.int32), ny, nx)
            hz, hy, hx = 0.5 - pk[5:6, sl], 0.5 - pk[6:7, sl], 0.5 - pk[7:8, sl]
            sum_z = jnp.zeros_like(hz)
            sum_y = jnp.zeros_like(hz)
            sum_x = jnp.zeros_like(hz)
            for t in range(-REACH, REACH + 1):
                sum_z = sum_z + tap(t + hz)
                iy = first + cy + t
                sum_y = sum_y + jnp.where((iy >= 0) & (iy < total_y), tap(t + hy), 0.0)
                ix = cx + t
                sum_x = sum_x + jnp.where((ix >= 0) & (ix < nx), tap(t + hx), 0.0)
            iz = lax.broadcasted_iota(jnp.int32, (planes, CHUNK), 0) - HALO - brick * nz - cz
            wz_ref[:, sl] = jnp.where(jnp.abs(iz) <= REACH, tap(iz.astype(F32) + hz), 0.0) * (1.0 / sum_z)
            row = lax.broadcasted_iota(jnp.int32, (rows, CHUNK), 0) - HALO
            iy = row - cy
            ok = (jnp.abs(iy) <= REACH) & (row + first >= 0) & (row + first < total_y)
            wy_ref[:, sl] = jnp.where(ok, tap(iy.astype(F32) + hy), 0.0) * (1.0 / sum_y)
            ix = (lax.broadcasted_iota(jnp.int32, (nx, CHUNK), 0) - cx).astype(F32)
            wx = jnp.where(jnp.abs(ix) <= REACH, tap(ix + hx), 0.0) * (1.0 / sum_x)
            wx_ref[:, sl] = wx.astype(jnp.bfloat16)

    def deposit(pk, lo, hi, add):
        def body(i, carry):
            acc = None
            for at in range(0, slots, CHUNK):
                sl = pl.ds(at, CHUNK)
                scaled = pk[0:4, sl] * wz_ref[pl.ds(i, 1), sl]
                wy = wy_ref[:, sl]
                lhs = jnp.concatenate([scaled[k : k + 1] * wy for k in range(4)], axis=0).astype(jnp.bfloat16)
                part = lax.dot_general(
                    lhs, wx_ref[:, sl], (((1,), (1,)), ((), ())), preferred_element_type=F32
                )
                acc = part if acc is None else acc + part
            acc = acc.reshape(4, rows, nx)
            dep[i] = dep[i] + acc if add else acc
            return carry

        lax.fori_loop(lo, hi, body, 0)

    dep[0] = jnp.zeros((4, rows, nx), F32)
    dep[planes - 1] = jnp.zeros((4, rows, nx), F32)
    prepare(pk_ref, 0)
    deposit(pk_ref, HALO - REACH, planes - (HALO - REACH), False)
    for c in near_copies:
        c.wait()

    def tile_copies(half):
        part = pl.ds(half * (planes // 2), planes // 2)
        north = remote(
            dep.at[part, :, pl.ds(ny, EDGE), :], tile_in.at[0, part], tile_send.at[half, 0],
            tile_recv.at[half, 0], {"gy": lax.rem(gy + 1, ngy)},
        )
        south = remote(
            dep.at[part, :, pl.ds(0, EDGE), :], tile_in.at[1, part], tile_send.at[half, 1],
            tile_recv.at[half, 1], {"gy": lax.rem(gy + ngy - 1, ngy)},
        )
        return [], north, south

    prepare(near.at[0], -1)
    deposit(near.at[0], 0, HALO + REACH, True)
    tiles0, tiles1 = tile_copies(0), tile_copies(1)
    halo_start(tiles0)
    prepare(near.at[1], 1)
    deposit(near.at[1], planes - HALO - REACH, planes, True)
    halo_start(tiles1)
    halo_wait(tiles0)
    halo_wait(tiles1)

    @pl.when(has_s)
    def _():
        dep[:, :, 0:EDGE, :] = dep[:, :, 0:EDGE, :] + tile_in[0]

    @pl.when(has_n)
    def _():
        dep[:, :, ny : ny + EDGE, :] = dep[:, :, ny : ny + EDGE, :] + tile_in[1]

    def shifts_x(v):
        lane = lax.broadcasted_iota(jnp.int32, v.shape, 1)
        west = jnp.where(lane > 0, pltpu.roll(v, 1, 1), 0.0)
        east = jnp.where(lane < nx - 1, pltpu.roll(v, nx - 1, 1), 0.0)
        return west, east

    def sweep(src, dst, lo, hi):
        place = lax.broadcasted_iota(jnp.int32, (rows, nx), 0) - HALO + first
        lane = lax.broadcasted_iota(jnp.int32, (rows, nx), 1)
        count = (
            2.0
            + (place >= 1).astype(F32)
            + (place < total_y - 1).astype(F32)
            + (lane >= 1).astype(F32)
            + (lane < nx - 1).astype(F32)
        )
        inside = (place >= 0) & (place < total_y)
        scale_c = jnp.where(inside, 1.0 - smooth_rate * count, 0.0)
        scale_n = jnp.where(inside, smooth_rate, 0.0)

        def body(i, carry):
            for k in range(4):
                c = src[i, k]
                west, east = shifts_x(c)
                beside = (
                    src[i - 1, k] + src[i + 1, k] + pltpu.roll(c, 1, 0) + pltpu.roll(c, rows - 1, 0) + west + east
                )
                dst[i, k] = scale_c * c + scale_n * beside
            return carry

        lax.fori_loop(lo, hi, body, 0)

    bufs = [dep, fld]
    for s in range(SWEEPS):
        sweep(bufs[s % 2], bufs[(s + 1) % 2], s + 1, planes - s - 1)
    f = bufs[SWEEPS % 2]

    def own(v, shift=0):
        return pltpu.roll(v, rows - HALO - shift, 0)[0:ny]

    halo_wait(pair_d)
    halo_wait(pair_p)
    for z in range(-1, nz + 1):
        g = own(1.0 / (1.0 + f[z + HALO, 0]))
        if 0 <= z < nz:
            gf_ref[z] = g
            for k in range(3):
                mom_ref[z, k] = own(f[z + HALO, k + 1])
            den = den_ref[z]
        else:
            den = halo_z[1, 0 if z < 0 else 1]
        mob[z + 1] = g / den

    row_id = lax.broadcasted_iota(jnp.int32, (ny, nx), 0)

    def shifts_y(v, south_row, north_row):
        south = jnp.where(row_id == 0, south_row, pltpu.roll(v, 1, 0))
        north = jnp.where(row_id == ny - 1, north_row, pltpu.roll(v, ny - 1, 0))
        return south, north

    def halo_rows(slot, z):
        s = jnp.where(has_s, halo_y[slot, 0, z, 7:8, :], 0.0)
        n = jnp.where(has_n, halo_y[slot, 1, z, 0:1, :], 0.0)
        return s, n

    def apply(v, slot, z):
        c = v[z]
        below = v[z - 1] if z > 0 else halo_z[slot, 0]
        above = v[z + 1] if z < nz - 1 else halo_z[slot, 1]
        south, north = shifts_y(c, *halo_rows(slot, z))
        west, east = shifts_x(c)
        coupled = (
            face_z[z] * below + face_z[z + 1] * above + face_s[z] * south + face_n[z] * north
            + face_w[z] * west + face_e[z] * east
        )
        return diag[z] * c - coupled

    for z in range(nz + 1):
        face_z[z] = 0.5 * (mob[z] + mob[z + 1])
    for z in range(nz):
        m = mob[z + 1]
        gs = f[z + HALO, 0, HALO - 1 : HALO, :]
        gn = f[z + HALO, 0, HALO + ny : HALO + ny + 1, :]
        ms = jnp.where(has_s, 1.0 / (1.0 + gs) / halo_y[1, 0, z, 7:8, :], 0.0)
        mn = jnp.where(has_n, 1.0 / (1.0 + gn) / halo_y[1, 1, z, 0:1, :], 0.0)
        south, north = shifts_y(m, ms, mn)
        west, east = shifts_x(m)
        fs, fn, fw, fe = 0.5 * (m + south), 0.5 * (m + north), 0.5 * (m + west), 0.5 * (m + east)
        face_s[z], face_n[z], face_w[z], face_e[z] = fs, fn, fw, fe
        dg = stiffness * m + face_z[z] + face_z[z + 1] + fs + fn + fw + fe
        diag[z] = dg
        mz_d, mz_u = own(f[z + HALO - 1, 1]), own(f[z + HALO + 1, 1])
        my = f[z + HALO, 2]
        xw, xe = shifts_x(own(f[z + HALO, 3]))
        spread = 0.5 * (mz_u - mz_d) + 0.5 * (own(my, 1) - own(my, -1)) + 0.5 * (xe - xw)
        r0 = div_ref[z] - spread - apply(p_ref, 0, z)
        r_ref[z] = r0
        z_ref[z] = r0 / dg

    pair_z = halo_pair(2, z_ref)
    halo_start(pair_z)
    halo_wait(pair_z)

    def fold(v):
        part = jnp.sum(v, axis=0, keepdims=True)
        out = part[:, 0:128]
        for at in range(128, nx, 128):
            out = out + part[:, at : at + 128]
        return out

    def reduce_y(n, a, b):
        ids = lax.broadcasted_iota(jnp.int32, (8, 128), 0)
        tile_y[n] = jnp.where(ids == 0, a, jnp.where(ids == 1, b, 0.0))
        copies = [
            remote(
                tile_y.at[n], red_y.at[n, d - 1], ry_send.at[n, d - 1], ry_recv.at[n, d - 1],
                {"gy": lax.rem(gy + d, ngy)},
            )
            for d in range(1, ngy)
        ]
        for c in copies:
            c.start()
        return copies

    def reduce_z(n, copies):
        for c in copies:
            c.wait()
        total = tile_y[n]
        for d in range(1, ngy):
            total = total + red_y[n, d - 1]
        tile_z[n] = total
        copies = [
            remote(
                tile_z.at[n], red_z.at[n, d - 1], rz_send.at[n, d - 1], rz_recv.at[n, d - 1],
                {"gz": lax.rem(gz + d, ngz)},
            )
            for d in range(1, ngz)
        ]
        for c in copies:
            c.start()
        return copies

    def reduce_end(n, copies):
        for c in copies:
            c.wait()
        total = tile_z[n]
        for d in range(1, ngz):
            total = total + red_z[n, d - 1]
        total = jnp.sum(total, axis=1, keepdims=True)
        return total[0:1], total[1:2]

    acc_a = acc_b = jnp.zeros((ny, nx), F32)
    for z in range(nz):
        q = apply(z_ref, 2, z)
        q_ref[z] = q
        w_ref[z] = q / diag[z]
        acc_a = acc_a + r_ref[z] * z_ref[z]
        acc_b = acc_b + z_ref[z] * q
    copies = reduce_y(0, fold(acc_a), fold(acc_b))
    pair_w = halo_pair(3, w_ref)
    halo_start(pair_w)
    copies = reduce_z(0, copies)
    halo_wait(pair_w)
    for z in range(nz):
        aw_ref[z] = apply(w_ref, 3, z)
    norm0, curve0 = reduce_end(0, copies)
    step0 = norm0 / curve0
    acc_a = acc_b = jnp.zeros((ny, nx), F32)
    for z in range(nz):
        r1 = r_ref[z] - step0 * q_ref[z]
        res_ref[z] = r1
        z1 = r1 / diag[z]
        az1 = q_ref[z] - step0 * aw_ref[z]
        acc_a = acc_a + r1 * z1
        acc_b = acc_b + z1 * az1
        w_ref[z] = z1
        aw_ref[z] = az1
    copies = reduce_z(1, reduce_y(1, fold(acc_a), fold(acc_b)))
    norm1, curve1 = reduce_end(1, copies)
    beta = norm1 / norm0
    step1 = norm1 / (curve1 - beta * norm1 / step0)
    for z in range(nz):
        d0 = z_ref[z]
        out_ref[z] = p_ref[z] + step0 * d0 + step1 * (w_ref[z] + beta * d0)
        res_ref[z] = res_ref[z] - step1 * (aw_ref[z] + beta * q_ref[z])


def on_device(ngz, ngy, parcel_cell, parcel_offset, parcel_volume, parcel_force, brick_counts,
              divergence, pressure_prev, gas_density):
    nz, ny, nx = divergence.shape
    slots = parcel_cell.shape[0]
    live = jnp.arange(slots, dtype=jnp.int32) < brick_counts[0, 0]
    volume = jnp.where(live, parcel_volume, 0.0)[None, :]
    packed = jnp.concatenate(
        [volume, volume * parcel_force, parcel_cell.astype(F32)[None, :], parcel_offset], axis=0
    )
    planes, rows = nz + 2 * HALO, ny + EDGE
    field = jax.ShapeDtypeStruct((nz, ny, nx), F32)
    own = pltpu.VMEM((nz, ny, nx), F32)
    dma = pltpu.SemaphoreType.DMA
    vmem = pl.BlockSpec(memory_space=pltpu.VMEM)
    return pl.pallas_call(
        functools.partial(step_kernel, ngz, ngy, nz, ny, nx, slots),
        out_shape=(field, jax.ShapeDtypeStruct((nz, 3, ny, nx), F32), field, field),
        in_specs=[vmem] * 4,
        out_specs=(vmem,) * 4,
        scratch_shapes=[
            pltpu.VMEM((2, 8, slots), F32),
            pltpu.VMEM((planes, slots), F32),
            pltpu.VMEM((rows, slots), F32),
            pltpu.VMEM((nx, slots), jnp.bfloat16),
            pltpu.VMEM((planes, 4, rows, nx), F32),
            pltpu.VMEM((planes, 4, rows, nx), F32),
            pltpu.VMEM((2, planes, 4, EDGE, nx), F32),
            pltpu.VMEM((4, 2, ny, nx), F32),
            pltpu.VMEM((4, 2, nz, 8, nx), F32),
            pltpu.VMEM((nz + 2, ny, nx), F32),
            pltpu.VMEM((nz + 1, ny, nx), F32),
            own, own, own, own, own,
            own, own, own, own, own,
            pltpu.VMEM((2, 8, 128), F32),
            pltpu.VMEM((2, 8, 128), F32),
            pltpu.VMEM((2, ngy - 1, 8, 128), F32),
            pltpu.VMEM((2, ngz - 1, 8, 128), F32),
            dma((2,)), dma((2,)),
            dma((2, 2)), dma((2, 2)),
            dma((4, 2)), dma((4, 2)), dma((4, 2)), dma((4, 2)),
            dma((2, ngy - 1)), dma((2, ngy - 1)), dma((2, ngz - 1)), dma((2, ngz - 1)),
        ],
        compiler_params=pltpu.CompilerParams(
            collective_id=0, has_side_effects=True, vmem_limit_bytes=60 * 1024 * 1024
        ),
    )(packed, divergence, pressure_prev, gas_density)


def solution(mesh):
    ngz, ngy = mesh.shape["gz"], mesh.shape["gy"]
    return jax.shard_map(
        functools.partial(on_device, ngz, ngy),
        mesh=mesh,
        in_specs=(
            P(("gz", "gy")),
            P(None, ("gz", "gy")),
            P(("gz", "gy")),
            P(None, ("gz", "gy")),
            P("gz", "gy"),
            P("gz", "gy", None),
            P("gz", "gy", None),
            P("gz", "gy", None),
        ),
        out_specs=(
            P("gz", "gy", None),
            P("gz", None, "gy", None),
            P("gz", "gy", None),
            P("gz", "gy", None),
        ),
        check_vma=False,
    )
```

```python
import functools
import math

import jax
import jax.numpy as jnp
from jax import lax
from jax.experimental import pallas as pl
from jax.experimental.pallas import tpu as pltpu
from jax.sharding import PartitionSpec as P

SWEEPS = 3
REACH = 3
HALO = SWEEPS + 1
EDGE = 2 * HALO
CHUNK = 1024
LANES = 128
PIECES = 4
smooth_rate = 0.15
stiffness = 0.002
F32 = jnp.float32
MESH = pl.DeviceIdType.MESH


def tap(distance):
    return jnp.exp2((-0.5 * math.log2(math.e)) * (distance * distance))


def split_cell(cell, ny, nx):
    if ny & (ny - 1) == 0 and nx & (nx - 1) == 0:
        sx, sy = nx.bit_length() - 1, ny.bit_length() - 1
        return (
            lax.shift_right_logical(cell, sx + sy),
            lax.shift_right_logical(cell, sx) & (ny - 1),
            cell & (nx - 1),
        )
    row = lax.div(cell, nx)
    return lax.div(row, ny), lax.rem(row, ny), lax.rem(cell, nx)


def step_kernel(
    ngz, ngy, nz, ny, nx, slots,
    count_ref, cell_ref, off_ref, vol_ref, force_ref, div_ref, p_ref, den_ref,
    gf_out, mom_out, p_out, res_out,
    gf_ref, mom_ref, out_ref, res_ref, pk_ref, near, wz_ref, wy_ref, wx_ref, dep, fld, tile_in,
    halo_z, halo_y, mob, face_z, face_s, face_n, face_w, face_e, diag,
    r_ref, z_ref, q_ref, w_ref, aw_ref, tile_y, tile_z, red_y, red_z,
    near_send, near_recv, tile_send, tile_recv, hz_send, hz_recv, hy_send, hy_recv,
    ry_send, ry_recv, rz_send, rz_recv, out_sem,
):
    gz, gy = lax.axis_index("gz"), lax.axis_index("gy")
    planes, rows = nz + 2 * HALO, ny + EDGE
    total_y = ngy * ny
    first = gy * ny
    up, down = lax.rem(gz + 1, ngz), lax.rem(gz + ngz - 1, ngz)
    has_s, has_n = gy > 0, gy < ngy - 1

    barrier = pltpu.get_barrier_semaphore()
    for d in range(1, ngz):
        pl.semaphore_signal(barrier, inc=1, device_id={"gz": lax.rem(gz + d, ngz)}, device_id_type=MESH)
    for d in range(1, ngy):
        pl.semaphore_signal(barrier, inc=1, device_id={"gy": lax.rem(gy + d, ngy)}, device_id_type=MESH)
    live = lax.broadcasted_iota(jnp.int32, (1, slots), 1) < count_ref[0, 0]
    volume = jnp.where(live, vol_ref[...], 0.0)
    pk_ref[0:1] = volume
    pk_ref[1:4] = volume * force_ref[...]
    pk_ref[4:5] = cell_ref[...].astype(F32)
    pk_ref[5:8] = off_ref[...]
    pl.semaphore_wait(barrier, ngz - 1 + ngy - 1)

    def remote(src, dst, send, recv, where):
        return pltpu.make_async_remote_copy(
            src_ref=src, dst_ref=dst, send_sem=send, recv_sem=recv, device_id=where, device_id_type=MESH
        )

    near_copies = [
        remote(pk_ref, near.at[0], near_send.at[0], near_recv.at[0], {"gz": up}),
        remote(pk_ref, near.at[1], near_send.at[1], near_recv.at[1], {"gz": down}),
    ]
    for c in near_copies:
        c.start()

    def halo_pair(slot, src):
        zc = [
            remote(src.at[nz - 1], halo_z.at[slot, 0], hz_send.at[slot, 0], hz_recv.at[slot, 0], {"gz": up}),
            remote(src.at[0], halo_z.at[slot, 1], hz_send.at[slot, 1], hz_recv.at[slot, 1], {"gz": down}),
        ]
        north = remote(
            src.at[:, pl.ds(ny - 8, 8), :], halo_y.at[slot, 0], hy_send.at[slot, 0], hy_recv.at[slot, 0],
            {"gy": lax.rem(gy + 1, ngy)},
        )
        south = remote(
            src.at[:, pl.ds(0, 8), :], halo_y.at[slot, 1], hy_send.at[slot, 1], hy_recv.at[slot, 1],
            {"gy": lax.rem(gy + ngy - 1, ngy)},
        )
        return zc, north, south

    def halo_start(pair, along_z=True):
        zc, north, south = pair
        for c in zc if along_z else []:
            c.start()

        @pl.when(has_n)
        def _():
            north.start()

        @pl.when(has_s)
        def _():
            south.start()

    def halo_wait(pair):
        zc, north, south = pair
        for c in zc:
            c.wait()

        @pl.when(has_n)
        def _():
            north.wait_send()
            south.wait_recv()

        @pl.when(has_s)
        def _():
            south.wait_send()
            north.wait_recv()

    pair_p, pair_d = halo_pair(0, p_ref), halo_pair(1, den_ref)
    halo_start(pair_d)
    halo_start(pair_p)

    row_iota = lax.broadcasted_iota(jnp.int32, (rows, LANES), 0) - HALO
    row_id = jnp.where((row_iota + first >= 0) & (row_iota + first < total_y), row_iota, 4 * total_y).astype(F32)
    col_id = lax.broadcasted_iota(jnp.int32, (nx, LANES), 0).astype(F32)
    plane_id = (lax.broadcasted_iota(jnp.int32, (planes, LANES), 0) - HALO).astype(F32)

    def prepare(pk, brick, slot, at, width):
        for off in range(0, width, LANES):
            sl = pl.ds(pl.multiple_of(at + off, LANES), LANES)
            cz, cy, cx = [c.astype(F32) for c in split_cell(pk[4:5, sl].astype(jnp.int32), ny, nx)]
            hz, hy, hx = 0.5 - pk[5:6, sl], 0.5 - pk[6:7, sl], 0.5 - pk[7:8, sl]
            sum_z = jnp.zeros_like(hz)
            for t in range(-REACH, REACH + 1):
                sum_z = sum_z + tap(t + hz)

            def masked(ids, home, half):
                t = ids - home
                return jnp.where(jnp.abs(t) <= REACH, tap(t + half), 0.0)

            wz_ref[slot, :, sl] = masked(plane_id - brick * nz, cz, hz) * (1.0 / sum_z)
            wy = masked(row_id, cy, hy)
            wy_ref[slot, :, sl] = wy * (1.0 / jnp.sum(wy, axis=0, keepdims=True))
            wx = masked(col_id, cx, hx)
            wx_ref[slot, :, sl] = (wx * (1.0 / jnp.sum(wx, axis=0, keepdims=True))).astype(jnp.bfloat16)

    def deposit(pk, slot, lo, hi, add, beside=None):
        def body(i, carry):
            acc = None
            for at in range(0, slots, CHUNK):
                sl = pl.ds(at, CHUNK)
                scaled = pk[0:4, sl] * wz_ref[slot, pl.ds(i, 1), sl]
                wy = wy_ref[slot, :, sl]
                lhs = jnp.concatenate([scaled[k : k + 1] * wy for k in range(4)], axis=0).astype(jnp.bfloat16)
                part = lax.dot_general(
                    lhs, wx_ref[slot, :, sl], (((1,), (1,)), ((), ())), preferred_element_type=F32
                )
                acc = part if acc is None else acc + part
            if beside is not None:
                beside(i - lo)
            acc = acc.reshape(4, rows, nx)
            dep[i] = dep[i] + acc if add else acc
            return carry

        lax.fori_loop(lo, hi, body, 0)

    dep[0] = jnp.zeros((4, rows, nx), F32)
    dep[planes - 1] = jnp.zeros((4, rows, nx), F32)
    piece = slots // nz

    def prepare_own(i, carry):
        prepare(pk_ref, 0, 0, i * piece, piece)
        return carry

    lax.fori_loop(0, nz, prepare_own, 0)

    def prepare_near(i):
        prepare(near.at[0], -1, 1, i * piece, piece)
        prepare(near.at[1], 1, 2, i * piece, piece)

    split_at = planes - (HALO - REACH) - nz
    deposit(pk_ref, 0, HALO - REACH, split_at, False)
    for c in near_copies:
        c.wait()
    deposit(pk_ref, 0, split_at, planes - (HALO - REACH), False, prepare_near)

    def tile_copies(half):
        part = pl.ds(half * (planes // 2), planes // 2)
        north = remote(
            dep.at[part, :, pl.ds(ny, EDGE), :], tile_in.at[0, part], tile_send.at[half, 0],
            tile_recv.at[half, 0], {"gy": lax.rem(gy + 1, ngy)},
        )
        south = remote(
            dep.at[part, :, pl.ds(0, EDGE), :], tile_in.at[1, part], tile_send.at[half, 1],
            tile_recv.at[half, 1], {"gy": lax.rem(gy + ngy - 1, ngy)},
        )
        return [], north, south

    deposit(near.at[0], 1, 0, HALO + REACH, True)
    tiles0, tiles1 = tile_copies(0), tile_copies(1)
    halo_start(tiles0)
    deposit(near.at[1], 2, planes - HALO - REACH, planes, True)
    halo_start(tiles1)

    def add_tiles(half):
        part = pl.ds(half * (planes // 2), planes // 2)

        @pl.when(has_s)
        def _():
            dep[part, :, 0:EDGE, :] = dep[part, :, 0:EDGE, :] + tile_in[0, part]

        @pl.when(has_n)
        def _():
            dep[part, :, ny : ny + EDGE, :] = dep[part, :, ny : ny + EDGE, :] + tile_in[1, part]

    def shifts_x(v):
        lane = lax.broadcasted_iota(jnp.int32, (v.shape[0], LANES), 1)
        parts = [v[:, at : at + LANES] for at in range(0, nx, LANES)]
        ups = [pltpu.roll(part, 1, 1) for part in parts]
        downs = [pltpu.roll(part, LANES - 1, 1) for part in parts]
        west = [jnp.where(lane == 0, ups[n - 1] if n else 0.0, u) for n, u in enumerate(ups)]
        east = [
            jnp.where(lane == LANES - 1, downs[n + 1] if n + 1 < len(parts) else 0.0, u) for n, u in enumerate(downs)
        ]
        return jnp.concatenate(west, axis=1), jnp.concatenate(east, axis=1)

    def sweep(src, dst, lo, hi):
        place = lax.broadcasted_iota(jnp.int32, (rows, nx), 0) - HALO + first
        lane = lax.broadcasted_iota(jnp.int32, (rows, nx), 1)
        count = (
            2.0
            + (place >= 1).astype(F32)
            + (place < total_y - 1).astype(F32)
            + (lane >= 1).astype(F32)
            + (lane < nx - 1).astype(F32)
        )
        inside = (place >= 0) & (place < total_y)
        scale_c = jnp.where(inside, 1.0 - smooth_rate * count, 0.0)
        scale_n = jnp.where(inside, smooth_rate, 0.0)

        def body(i, carry):
            for k in range(4):
                c = src[i, k]
                west, east = shifts_x(c)
                beside = (
                    src[i - 1, k] + src[i + 1, k] + pltpu.roll(c, 1, 0) + pltpu.roll(c, rows - 1, 0) + west + east
                )
                dst[i, k] = scale_c * c + scale_n * beside
            return carry

        lax.fori_loop(lo, hi, body, 0)

    bufs = [dep, fld]
    halo_wait(tiles0)
    add_tiles(0)
    sweep(dep, fld, 1, planes // 2 - 1)
    halo_wait(tiles1)
    add_tiles(1)
    sweep(dep, fld, planes // 2 - 1, planes - 1)
    for s in range(1, SWEEPS):
        sweep(bufs[s % 2], bufs[(s + 1) % 2], s + 1, planes - s - 1)
    f = bufs[SWEEPS % 2]

    def own(v, shift=0):
        return pltpu.roll(v, rows - HALO - shift, 0)[0:ny]

    halo_wait(pair_d)
    halo_wait(pair_p)
    for z in range(-1, nz + 1):
        g = own(1.0 / (1.0 + f[z + HALO, 0]))
        if 0 <= z < nz:
            gf_ref[z] = g
            for k in range(3):
                mom_ref[z, k] = own(f[z + HALO, k + 1])
            den = den_ref[z]
        else:
            den = halo_z[1, 0 if z < 0 else 1]
        mob[z + 1] = g / den

    early = [
        pltpu.make_async_copy(gf_ref, gf_out, out_sem.at[0]),
        pltpu.make_async_copy(mom_ref, mom_out, out_sem.at[1]),
    ]
    for c in early:
        c.start()
    own_row = lax.broadcasted_iota(jnp.int32, (ny, nx), 0)

    def shifts_y(v, south_row, north_row):
        south = jnp.where(own_row == 0, south_row, pltpu.roll(v, 1, 0))
        north = jnp.where(own_row == ny - 1, north_row, pltpu.roll(v, ny - 1, 0))
        return south, north

    def halo_rows(slot, z):
        s = jnp.where(has_s, halo_y[slot, 0, z, 7:8, :], 0.0)
        n = jnp.where(has_n, halo_y[slot, 1, z, 0:1, :], 0.0)
        return s, n

    def apply(v, slot, z):
        c = v[z]
        below = v[z - 1] if z > 0 else halo_z[slot, 0]
        above = v[z + 1] if z < nz - 1 else halo_z[slot, 1]
        south, north = shifts_y(c, *halo_rows(slot, z))
        west, east = shifts_x(c)
        coupled = (
            face_z[z] * below + face_z[z + 1] * above + face_s[z] * south + face_n[z] * north
            + face_w[z] * west + face_e[z] * east
        )
        return diag[z] * c - coupled

    for z in range(nz + 1):
        face_z[z] = 0.5 * (mob[z] + mob[z + 1])
    order = [0, nz - 1] + list(range(1, nz - 1))
    pair_z, pair_w = halo_pair(2, z_ref), halo_pair(3, w_ref)
    for z in order:
        m = mob[z + 1]
        gs = f[z + HALO, 0, HALO - 1 : HALO, :]
        gn = f[z + HALO, 0, HALO + ny : HALO + ny + 1, :]
        ms = jnp.where(has_s, 1.0 / (1.0 + gs) / halo_y[1, 0, z, 7:8, :], 0.0)
        mn = jnp.where(has_n, 1.0 / (1.0 + gn) / halo_y[1, 1, z, 0:1, :], 0.0)
        south, north = shifts_y(m, ms, mn)
        west, east = shifts_x(m)
        fs, fn, fw, fe = 0.5 * (m + south), 0.5 * (m + north), 0.5 * (m + west), 0.5 * (m + east)
        face_s[z], face_n[z], face_w[z], face_e[z] = fs, fn, fw, fe
        dg = stiffness * m + face_z[z] + face_z[z + 1] + fs + fn + fw + fe
        diag[z] = dg
        mz_d, mz_u = own(f[z + HALO - 1, 1]), own(f[z + HALO + 1, 1])
        my = f[z + HALO, 2]
        xw, xe = shifts_x(own(f[z + HALO, 3]))
        spread = 0.5 * (mz_u - mz_d) + 0.5 * (own(my, 1) - own(my, -1)) + 0.5 * (xe - xw)
        r0 = div_ref[z] - spread - apply(p_ref, 0, z)
        r_ref[z] = r0
        z_ref[z] = r0 / dg
        if z == nz - 1:
            for c in pair_z[0]:
                c.start()

    halo_start(pair_z, False)
    halo_wait(pair_z)

    def fold(v):
        part = jnp.sum(v, axis=0, keepdims=True)
        out = part[:, 0:128]
        for at in range(128, nx, 128):
            out = out + part[:, at : at + 128]
        return out

    def reduce_y(n, a, b):
        ids = lax.broadcasted_iota(jnp.int32, (8, 128), 0)
        tile_y[n] = jnp.where(ids == 0, a, jnp.where(ids == 1, b, 0.0))
        copies = [
            remote(
                tile_y.at[n], red_y.at[n, d - 1], ry_send.at[n, d - 1], ry_recv.at[n, d - 1],
                {"gy": lax.rem(gy + d, ngy)},
            )
            for d in range(1, ngy)
        ]
        for c in copies:
            c.start()
        return copies

    def reduce_z(n, copies):
        for c in copies:
            c.wait()
        total = tile_y[n]
        for d in range(1, ngy):
            total = total + red_y[n, d - 1]
        tile_z[n] = total
        copies = [
            remote(
                tile_z.at[n], red_z.at[n, d - 1], rz_send.at[n, d - 1], rz_recv.at[n, d - 1],
                {"gz": lax.rem(gz + d, ngz)},
            )
            for d in range(1, ngz)
        ]
        for c in copies:
            c.start()
        return copies

    def reduce_end(n, copies):
        for c in copies:
            c.wait()
        total = tile_z[n]
        for d in range(1, ngz):
            total = total + red_z[n, d - 1]
        total = jnp.sum(total, axis=1, keepdims=True)
        return total[0:1], total[1:2]

    acc_a = acc_b = jnp.zeros((ny, nx), F32)
    for z in order:
        q = apply(z_ref, 2, z)
        q_ref[z] = q
        w_ref[z] = q / diag[z]
        if z == nz - 1:
            for c in pair_w[0]:
                c.start()
        acc_a = acc_a + r_ref[z] * z_ref[z]
        acc_b = acc_b + z_ref[z] * q
    copies = reduce_y(0, fold(acc_a), fold(acc_b))
    halo_start(pair_w, False)
    copies = reduce_z(0, copies)
    halo_wait(pair_w)
    for z in range(nz):
        aw_ref[z] = apply(w_ref, 3, z)
    norm0, curve0 = reduce_end(0, copies)
    step0 = norm0 / curve0
    acc_a = acc_b = jnp.zeros((ny, nx), F32)
    for z in range(nz):
        r1 = r_ref[z] - step0 * q_ref[z]
        res_ref[z] = r1
        z1 = r1 / diag[z]
        az1 = q_ref[z] - step0 * aw_ref[z]
        acc_a = acc_a + r1 * z1
        acc_b = acc_b + z1 * az1
        w_ref[z] = z1
        aw_ref[z] = az1
    copies = reduce_z(1, reduce_y(1, fold(acc_a), fold(acc_b)))
    norm1, curve1 = reduce_end(1, copies)
    beta = norm1 / norm0
    step1 = norm1 / (curve1 - beta * norm1 / step0)
    for z in range(nz):
        d0 = z_ref[z]
        out_ref[z] = p_ref[z] + step0 * d0 + step1 * (w_ref[z] + beta * d0)
        res_ref[z] = res_ref[z] - step1 * (aw_ref[z] + beta * q_ref[z])
    late = [
        pltpu.make_async_copy(out_ref, p_out, out_sem.at[2]),
        pltpu.make_async_copy(res_ref, res_out, out_sem.at[3]),
    ]
    for c in late:
        c.start()
    for c in early + late:
        c.wait()


def pass_kernel(*refs):
    ins, outs, bufs, (got, put) = refs[0:4], refs[4:8], refs[8:12], refs[12:]
    ways = []
    for n in range(4):
        size = ins[n].shape[0] // PIECES
        for h in range(PIECES):
            part = pl.ds(h * size, size)
            ways.append((
                pltpu.make_async_copy(ins[n].at[part], bufs[n].at[part], got.at[n, h]),
                pltpu.make_async_copy(bufs[n].at[part], outs[n].at[part], put.at[n, h]),
            ))
    for first, _ in ways:
        first.start()
    for first, second in ways:
        first.wait()
        second.start()
    for _, second in ways:
        second.wait()


def on_device(ngz, ngy, parcel_cell, parcel_offset, parcel_volume, parcel_force, brick_counts,
              divergence, pressure_prev, gas_density):
    nz, ny, nx = divergence.shape
    slots = parcel_cell.shape[0]
    planes, rows = nz + 2 * HALO, ny + EDGE
    field = jax.ShapeDtypeStruct((nz, ny, nx), F32)
    own = pltpu.VMEM((nz, ny, nx), F32)
    dma = pltpu.SemaphoreType.DMA
    vmem = pl.BlockSpec(memory_space=pltpu.VMEM)
    hbm = pl.BlockSpec(memory_space=pl.ANY)
    shapes = (field, jax.ShapeDtypeStruct((nz, 3, ny, nx), F32), field, field)
    bufs = [pltpu.VMEM(shape.shape, F32) for shape in shapes]
    made = pl.pallas_call(
        functools.partial(step_kernel, ngz, ngy, nz, ny, nx, slots),
        out_shape=shapes,
        in_specs=[pl.BlockSpec(memory_space=pltpu.SMEM)] + [vmem] * 7,
        out_specs=(hbm,) * 4,
        scratch_shapes=bufs + [
            pltpu.VMEM((8, slots), F32),
            pltpu.VMEM((2, 8, slots), F32),
            pltpu.VMEM((3, planes, slots), F32),
            pltpu.VMEM((3, rows, slots), F32),
            pltpu.VMEM((3, nx, slots), jnp.bfloat16),
            pltpu.VMEM((planes, 4, rows, nx), F32),
            pltpu.VMEM((planes, 4, rows, nx), F32),
            pltpu.VMEM((2, planes, 4, EDGE, nx), F32),
            pltpu.VMEM((4, 2, ny, nx), F32),
            pltpu.VMEM((4, 2, nz, 8, nx), F32),
            pltpu.VMEM((nz + 2, ny, nx), F32),
            pltpu.VMEM((nz + 1, ny, nx), F32),
            own, own, own, own, own,
            own, own, own, own, own,
            pltpu.VMEM((2, 8, 128), F32),
            pltpu.VMEM((2, 8, 128), F32),
            pltpu.VMEM((2, ngy - 1, 8, 128), F32),
            pltpu.VMEM((2, ngz - 1, 8, 128), F32),
            dma((2,)), dma((2,)),
            dma((2, 2)), dma((2, 2)),
            dma((4, 2)), dma((4, 2)), dma((4, 2)), dma((4, 2)),
            dma((2, ngy - 1)), dma((2, ngy - 1)), dma((2, ngz - 1)), dma((2, ngz - 1)), dma((4,)),
        ],
        compiler_params=pltpu.CompilerParams(
            collective_id=0, has_side_effects=True, vmem_limit_bytes=60 * 1024 * 1024
        ),
    )(
        brick_counts, parcel_cell[None, :], parcel_offset, parcel_volume[None, :], parcel_force,
        divergence, pressure_prev, gas_density,
    )
    return pl.pallas_call(
        pass_kernel,
        out_shape=shapes,
        in_specs=[hbm] * 4,
        out_specs=(hbm,) * 4,
        scratch_shapes=bufs + [dma((4, PIECES)), dma((4, PIECES))],
    )(*made)


def solution(mesh):
    ngz, ngy = mesh.shape["gz"], mesh.shape["gy"]
    return jax.shard_map(
        functools.partial(on_device, ngz, ngy),
        mesh=mesh,
        in_specs=(
            P(("gz", "gy")),
            P(None, ("gz", "gy")),
            P(("gz", "gy")),
            P(None, ("gz", "gy")),
            P("gz", "gy"),
            P("gz", "gy", None),
            P("gz", "gy", None),
            P("gz", "gy", None),
        ),
        out_specs=(
            P("gz", "gy", None),
            P("gz", None, "gy", None),
            P("gz", "gy", None),
            P("gz", "gy", None),
        ),
        check_vma=False,
    )
```

```python
import functools
import math

import jax
import jax.numpy as jnp
from jax import lax
from jax.experimental import pallas as pl
from jax.experimental.pallas import tpu as pltpu
from jax.sharding import PartitionSpec as P

SWEEPS = 3
REACH = 3
HALO = SWEEPS + 1
EDGE = 2 * HALO
CHUNK = 1024
LANES = 128
PIECES = 4
smooth_rate = 0.15
stiffness = 0.002
F32 = jnp.float32
MESH = pl.DeviceIdType.MESH


def tap(distance):
    return jnp.exp2((-0.5 * math.log2(math.e)) * (distance * distance))


def split_cell(cell, ny, nx):
    if ny & (ny - 1) == 0 and nx & (nx - 1) == 0:
        sx, sy = nx.bit_length() - 1, ny.bit_length() - 1
        return (
            lax.shift_right_logical(cell, sx + sy),
            lax.shift_right_logical(cell, sx) & (ny - 1),
            cell & (nx - 1),
        )
    row = lax.div(cell, nx)
    return lax.div(row, ny), lax.rem(row, ny), lax.rem(cell, nx)


def step_kernel(
    ngz, ngy, nz, ny, nx, slots,
    count_ref, cell_ref, off_ref, vol_ref, force_ref, div_ref, p_ref, den_ref,
    gf_out, mom_out, p_out, res_out,
    gf_ref, mom_ref, out_ref, res_ref, pk_ref, near, wz_ref, wy_ref, wx_ref, dep, fld, tile_in,
    halo_z, halo_y, mob, face_z, face_s, face_n, face_w, face_e, diag,
    r_ref, z_ref, q_ref, w_ref, aw_ref, tile_y, tile_z, red_y, red_z,
    near_send, near_recv, tile_send, tile_recv, hz_send, hz_recv, hy_send, hy_recv,
    ry_send, ry_recv, rz_send, rz_recv, out_sem,
):
    gz, gy = lax.axis_index("gz"), lax.axis_index("gy")
    planes, rows = nz + 2 * HALO, ny + EDGE
    total_y = ngy * ny
    first = gy * ny
    up, down = lax.rem(gz + 1, ngz), lax.rem(gz + ngz - 1, ngz)
    has_s, has_n = gy > 0, gy < ngy - 1

    barrier = pltpu.get_barrier_semaphore()
    for d in range(1, ngz):
        pl.semaphore_signal(barrier, inc=1, device_id={"gz": lax.rem(gz + d, ngz)}, device_id_type=MESH)
    for d in range(1, ngy):
        pl.semaphore_signal(barrier, inc=1, device_id={"gy": lax.rem(gy + d, ngy)}, device_id_type=MESH)
    live = lax.broadcasted_iota(jnp.int32, (1, slots), 1) < count_ref[0, 0]
    volume = jnp.where(live, vol_ref[...], 0.0)
    pk_ref[0:1] = volume
    pk_ref[1:4] = volume * force_ref[...]
    pk_ref[4:5] = cell_ref[...].astype(F32)
    pk_ref[5:8] = off_ref[...]
    pl.semaphore_wait(barrier, ngz - 1 + ngy - 1)

    def remote(src, dst, send, recv, where):
        return pltpu.make_async_remote_copy(
            src_ref=src, dst_ref=dst, send_sem=send, recv_sem=recv, device_id=where, device_id_type=MESH
        )

    near_copies = [
        remote(pk_ref, near.at[0], near_send.at[0], near_recv.at[0], {"gz": up}),
        remote(pk_ref, near.at[1], near_send.at[1], near_recv.at[1], {"gz": down}),
    ]
    for c in near_copies:
        c.start()

    def halo_pair(slot, src):
        zc = [
            remote(src.at[nz - 1], halo_z.at[slot, 0], hz_send.at[slot, 0], hz_recv.at[slot, 0], {"gz": up}),
            remote(src.at[0], halo_z.at[slot, 1], hz_send.at[slot, 1], hz_recv.at[slot, 1], {"gz": down}),
        ]
        north = remote(
            src.at[:, pl.ds(ny - 8, 8), :], halo_y.at[slot, 0], hy_send.at[slot, 0], hy_recv.at[slot, 0],
            {"gy": lax.rem(gy + 1, ngy)},
        )
        south = remote(
            src.at[:, pl.ds(0, 8), :], halo_y.at[slot, 1], hy_send.at[slot, 1], hy_recv.at[slot, 1],
            {"gy": lax.rem(gy + ngy - 1, ngy)},
        )
        return zc, north, south

    def halo_start(pair, along_z=True):
        zc, north, south = pair
        for c in zc if along_z else []:
            c.start()

        @pl.when(has_n)
        def _():
            north.start()

        @pl.when(has_s)
        def _():
            south.start()

    def halo_wait(pair):
        zc, north, south = pair
        for c in zc:
            c.wait()

        @pl.when(has_n)
        def _():
            north.wait_send()
            south.wait_recv()

        @pl.when(has_s)
        def _():
            south.wait_send()
            north.wait_recv()

    pair_p, pair_d = halo_pair(0, p_ref), halo_pair(1, den_ref)
    halo_start(pair_d)
    halo_start(pair_p)

    row_iota = lax.broadcasted_iota(jnp.int32, (rows, LANES), 0) - HALO
    row_id = jnp.where((row_iota + first >= 0) & (row_iota + first < total_y), row_iota, 4 * total_y).astype(F32)
    col_id = lax.broadcasted_iota(jnp.int32, (nx, LANES), 0).astype(F32)
    plane_id = (lax.broadcasted_iota(jnp.int32, (planes, LANES), 0) - HALO).astype(F32)

    def prepare(pk, brick, slot, at, width):
        for off in range(0, width, LANES):
            sl = pl.ds(pl.multiple_of(at + off, LANES), LANES)
            cz, cy, cx = [c.astype(F32) for c in split_cell(pk[4:5, sl].astype(jnp.int32), ny, nx)]
            hz, hy, hx = 0.5 - pk[5:6, sl], 0.5 - pk[6:7, sl], 0.5 - pk[7:8, sl]
            sum_z = jnp.zeros_like(hz)
            for t in range(-REACH, REACH + 1):
                sum_z = sum_z + tap(t + hz)

            def masked(ids, home, half):
                t = ids - home
                return jnp.where(jnp.abs(t) <= REACH, tap(t + half), 0.0)

            wz_ref[slot, :, sl] = masked(plane_id - brick * nz, cz, hz) * (1.0 / sum_z)
            wy = masked(row_id, cy, hy)
            wy_ref[slot, :, sl] = wy * (1.0 / jnp.sum(wy, axis=0, keepdims=True))
            wx = masked(col_id, cx, hx)
            wx_ref[slot, :, sl] = (wx * (1.0 / jnp.sum(wx, axis=0, keepdims=True))).astype(jnp.bfloat16)

    def deposit(pk, slot, lo, hi, add, beside=None):
        def body(i, carry):
            acc = None
            for at in range(0, slots, CHUNK):
                sl = pl.ds(at, CHUNK)
                scaled = pk[0:4, sl] * wz_ref[slot, pl.ds(i, 1), sl]
                wy = wy_ref[slot, :, sl]
                lhs = jnp.concatenate([scaled[k : k + 1] * wy for k in range(4)], axis=0).astype(jnp.bfloat16)
                part = lax.dot_general(
                    lhs, wx_ref[slot, :, sl], (((1,), (1,)), ((), ())), preferred_element_type=F32
                )
                acc = part if acc is None else acc + part
                if beside is not None:
                    beside(i - lo, at // CHUNK)
            acc = acc.reshape(4, rows, nx)
            dep[i] = dep[i] + acc if add else acc
            return carry

        lax.fori_loop(lo, hi, body, 0)

    dep[0] = jnp.zeros((4, rows, nx), F32)
    dep[planes - 1] = jnp.zeros((4, rows, nx), F32)
    piece = slots // nz

    def prepare_own(i, carry):
        prepare(pk_ref, 0, 0, i * piece, piece)
        return carry

    lax.fori_loop(0, nz, prepare_own, 0)

    share = piece // (slots // CHUNK)

    def prepare_near(i, n):
        prepare(near.at[0], -1, 1, i * piece + n * share, share)
        prepare(near.at[1], 1, 2, i * piece + n * share, share)

    split_at = planes - (HALO - REACH) - nz
    deposit(pk_ref, 0, HALO - REACH, split_at, False)
    for c in near_copies:
        c.wait()
    deposit(pk_ref, 0, split_at, planes - (HALO - REACH), False, prepare_near)

    def tile_copies(half):
        part = pl.ds(half * (planes // 2), planes // 2)
        north = remote(
            dep.at[part, :, pl.ds(ny, EDGE), :], tile_in.at[0, part], tile_send.at[half, 0],
            tile_recv.at[half, 0], {"gy": lax.rem(gy + 1, ngy)},
        )
        south = remote(
            dep.at[part, :, pl.ds(0, EDGE), :], tile_in.at[1, part], tile_send.at[half, 1],
            tile_recv.at[half, 1], {"gy": lax.rem(gy + ngy - 1, ngy)},
        )
        return [], north, south

    deposit(near.at[0], 1, 0, HALO + REACH, True)
    tiles0, tiles1 = tile_copies(0), tile_copies(1)
    halo_start(tiles0)
    deposit(near.at[1], 2, planes - HALO - REACH, planes, True)
    halo_start(tiles1)

    def add_tiles(half):
        part = pl.ds(half * (planes // 2), planes // 2)

        @pl.when(has_s)
        def _():
            dep[part, :, 0:EDGE, :] = dep[part, :, 0:EDGE, :] + tile_in[0, part]

        @pl.when(has_n)
        def _():
            dep[part, :, ny : ny + EDGE, :] = dep[part, :, ny : ny + EDGE, :] + tile_in[1, part]

    def shifts_x(v):
        lane = lax.broadcasted_iota(jnp.int32, (v.shape[0], LANES), 1)
        parts = [v[:, at : at + LANES] for at in range(0, nx, LANES)]
        ups = [pltpu.roll(part, 1, 1) for part in parts]
        downs = [pltpu.roll(part, LANES - 1, 1) for part in parts]
        west = [jnp.where(lane == 0, ups[n - 1] if n else 0.0, u) for n, u in enumerate(ups)]
        east = [
            jnp.where(lane == LANES - 1, downs[n + 1] if n + 1 < len(parts) else 0.0, u) for n, u in enumerate(downs)
        ]
        return jnp.concatenate(west, axis=1), jnp.concatenate(east, axis=1)

    def sweep(src, dst, lo, hi):
        place = lax.broadcasted_iota(jnp.int32, (rows, nx), 0) - HALO + first
        lane = lax.broadcasted_iota(jnp.int32, (rows, nx), 1)
        count = (
            2.0
            + (place >= 1).astype(F32)
            + (place < total_y - 1).astype(F32)
            + (lane >= 1).astype(F32)
            + (lane < nx - 1).astype(F32)
        )
        inside = (place >= 0) & (place < total_y)
        scale_c = jnp.where(inside, 1.0 - smooth_rate * count, 0.0)
        scale_n = jnp.where(inside, smooth_rate, 0.0)

        def body(i, carry):
            for k in range(4):
                c = src[i, k]
                west, east = shifts_x(c)
                beside = (
                    src[i - 1, k] + src[i + 1, k] + pltpu.roll(c, 1, 0) + pltpu.roll(c, rows - 1, 0) + west + east
                )
                dst[i, k] = scale_c * c + scale_n * beside
            return carry

        lax.fori_loop(lo, hi, body, 0)

    bufs = [dep, fld]
    halo_wait(tiles0)
    add_tiles(0)
    sweep(dep, fld, 1, planes // 2 - 1)
    halo_wait(tiles1)
    add_tiles(1)
    sweep(dep, fld, planes // 2 - 1, planes - 1)
    for s in range(1, SWEEPS):
        sweep(bufs[s % 2], bufs[(s + 1) % 2], s + 1, planes - s - 1)
    f = bufs[SWEEPS % 2]

    def own(v, shift=0):
        return pltpu.roll(v, rows - HALO - shift, 0)[0:ny]

    halo_wait(pair_d)
    halo_wait(pair_p)
    for z in range(-1, nz + 1):
        g = own(1.0 / (1.0 + f[z + HALO, 0]))
        if 0 <= z < nz:
            gf_ref[z] = g
            for k in range(3):
                mom_ref[z, k] = own(f[z + HALO, k + 1])
            den = den_ref[z]
        else:
            den = halo_z[1, 0 if z < 0 else 1]
        mob[z + 1] = g / den

    early = [
        pltpu.make_async_copy(gf_ref, gf_out, out_sem.at[0]),
        pltpu.make_async_copy(mom_ref, mom_out, out_sem.at[1]),
    ]
    for c in early:
        c.start()
    own_row = lax.broadcasted_iota(jnp.int32, (ny, nx), 0)

    def shifts_y(v, south_row, north_row):
        south = jnp.where(own_row == 0, south_row, pltpu.roll(v, 1, 0))
        north = jnp.where(own_row == ny - 1, north_row, pltpu.roll(v, ny - 1, 0))
        return south, north

    def halo_rows(slot, z):
        s = jnp.where(has_s, halo_y[slot, 0, z, 7:8, :], 0.0)
        n = jnp.where(has_n, halo_y[slot, 1, z, 0:1, :], 0.0)
        return s, n

    def apply(v, slot, z):
        c = v[z]
        below = v[z - 1] if z > 0 else halo_z[slot, 0]
        above = v[z + 1] if z < nz - 1 else halo_z[slot, 1]
        south, north = shifts_y(c, *halo_rows(slot, z))
        west, east = shifts_x(c)
        coupled = (
            face_z[z] * below + face_z[z + 1] * above + face_s[z] * south + face_n[z] * north
            + face_w[z] * west + face_e[z] * east
        )
        return diag[z] * c - coupled

    for z in range(nz + 1):
        face_z[z] = 0.5 * (mob[z] + mob[z + 1])
    order = [0, nz - 1] + list(range(1, nz - 1))
    pair_z, pair_w = halo_pair(2, z_ref), halo_pair(3, w_ref)
    for z in order:
        m = mob[z + 1]
        gs = f[z + HALO, 0, HALO - 1 : HALO, :]
        gn = f[z + HALO, 0, HALO + ny : HALO + ny + 1, :]
        ms = jnp.where(has_s, 1.0 / (1.0 + gs) / halo_y[1, 0, z, 7:8, :], 0.0)
        mn = jnp.where(has_n, 1.0 / (1.0 + gn) / halo_y[1, 1, z, 0:1, :], 0.0)
        south, north = shifts_y(m, ms, mn)
        west, east = shifts_x(m)
        fs, fn, fw, fe = 0.5 * (m + south), 0.5 * (m + north), 0.5 * (m + west), 0.5 * (m + east)
        face_s[z], face_n[z], face_w[z], face_e[z] = fs, fn, fw, fe
        dg = stiffness * m + face_z[z] + face_z[z + 1] + fs + fn + fw + fe
        diag[z] = dg
        mz_d, mz_u = own(f[z + HALO - 1, 1]), own(f[z + HALO + 1, 1])
        my = f[z + HALO, 2]
        xw, xe = shifts_x(own(f[z + HALO, 3]))
        spread = 0.5 * (mz_u - mz_d) + 0.5 * (own(my, 1) - own(my, -1)) + 0.5 * (xe - xw)
        r0 = div_ref[z] - spread - apply(p_ref, 0, z)
        r_ref[z] = r0
        z_ref[z] = r0 / dg
        if z == nz - 1:
            for c in pair_z[0]:
                c.start()

    halo_start(pair_z, False)
    halo_wait(pair_z)

    def fold(v):
        part = jnp.sum(v, axis=0, keepdims=True)
        out = part[:, 0:128]
        for at in range(128, nx, 128):
            out = out + part[:, at : at + 128]
        return out

    def reduce_y(n, a, b):
        ids = lax.broadcasted_iota(jnp.int32, (8, 128), 0)
        tile_y[n] = jnp.where(ids == 0, a, jnp.where(ids == 1, b, 0.0))
        copies = [
            remote(
                tile_y.at[n], red_y.at[n, d - 1], ry_send.at[n, d - 1], ry_recv.at[n, d - 1],
                {"gy": lax.rem(gy + d, ngy)},
            )
            for d in range(1, ngy)
        ]
        for c in copies:
            c.start()
        return copies

    def reduce_z(n, copies):
        for c in copies:
            c.wait()
        total = tile_y[n]
        for d in range(1, ngy):
            total = total + red_y[n, d - 1]
        tile_z[n] = total
        copies = [
            remote(
                tile_z.at[n], red_z.at[n, d - 1], rz_send.at[n, d - 1], rz_recv.at[n, d - 1],
                {"gz": lax.rem(gz + d, ngz)},
            )
            for d in range(1, ngz)
        ]
        for c in copies:
            c.start()
        return copies

    def reduce_end(n, copies):
        for c in copies:
            c.wait()
        total = tile_z[n]
        for d in range(1, ngz):
            total = total + red_z[n, d - 1]
        total = jnp.sum(total, axis=1, keepdims=True)
        return total[0:1], total[1:2]

    acc_a = acc_b = jnp.zeros((ny, nx), F32)
    for z in order:
        q = apply(z_ref, 2, z)
        q_ref[z] = q
        w_ref[z] = q / diag[z]
        if z == nz - 1:
            for c in pair_w[0]:
                c.start()
        acc_a = acc_a + r_ref[z] * z_ref[z]
        acc_b = acc_b + z_ref[z] * q
    copies = reduce_y(0, fold(acc_a), fold(acc_b))
    halo_start(pair_w, False)
    copies = reduce_z(0, copies)
    halo_wait(pair_w)
    for z in range(nz):
        aw_ref[z] = apply(w_ref, 3, z)
    norm0, curve0 = reduce_end(0, copies)
    step0 = norm0 / curve0
    acc_a = acc_b = jnp.zeros((ny, nx), F32)
    for z in range(nz):
        r1 = r_ref[z] - step0 * q_ref[z]
        res_ref[z] = r1
        z1 = r1 / diag[z]
        az1 = q_ref[z] - step0 * aw_ref[z]
        acc_a = acc_a + r1 * z1
        acc_b = acc_b + z1 * az1
        w_ref[z] = z1
        aw_ref[z] = az1
    copies = reduce_z(1, reduce_y(1, fold(acc_a), fold(acc_b)))
    norm1, curve1 = reduce_end(1, copies)
    beta = norm1 / norm0
    step1 = norm1 / (curve1 - beta * norm1 / step0)
    for z in range(nz):
        d0 = z_ref[z]
        out_ref[z] = p_ref[z] + step0 * d0 + step1 * (w_ref[z] + beta * d0)
        res_ref[z] = res_ref[z] - step1 * (aw_ref[z] + beta * q_ref[z])
    late = [
        pltpu.make_async_copy(out_ref, p_out, out_sem.at[2]),
        pltpu.make_async_copy(res_ref, res_out, out_sem.at[3]),
    ]
    for c in late:
        c.start()
    for c in early + late:
        c.wait()


def pass_kernel(*refs):
    ins, outs, bufs, (got, put) = refs[0:4], refs[4:8], refs[8:12], refs[12:]
    ways = []
    for n in range(4):
        size = ins[n].shape[0] // PIECES
        for h in range(PIECES):
            part = pl.ds(h * size, size)
            ways.append((
                pltpu.make_async_copy(ins[n].at[part], bufs[n].at[part], got.at[n, h]),
                pltpu.make_async_copy(bufs[n].at[part], outs[n].at[part], put.at[n, h]),
            ))
    for first, _ in ways:
        first.start()
    for first, second in ways:
        first.wait()
        second.start()
    for _, second in ways:
        second.wait()


def on_device(ngz, ngy, parcel_cell, parcel_offset, parcel_volume, parcel_force, brick_counts,
              divergence, pressure_prev, gas_density):
    nz, ny, nx = divergence.shape
    slots = parcel_cell.shape[0]
    planes, rows = nz + 2 * HALO, ny + EDGE
    field = jax.ShapeDtypeStruct((nz, ny, nx), F32)
    own = pltpu.VMEM((nz, ny, nx), F32)
    dma = pltpu.SemaphoreType.DMA
    vmem = pl.BlockSpec(memory_space=pltpu.VMEM)
    hbm = pl.BlockSpec(memory_space=pl.ANY)
    shapes = (field, jax.ShapeDtypeStruct((nz, 3, ny, nx), F32), field, field)
    bufs = [pltpu.VMEM(shape.shape, F32) for shape in shapes]
    made = pl.pallas_call(
        functools.partial(step_kernel, ngz, ngy, nz, ny, nx, slots),
        out_shape=shapes,
        in_specs=[pl.BlockSpec(memory_space=pltpu.SMEM)] + [vmem] * 7,
        out_specs=(hbm,) * 4,
        scratch_shapes=bufs + [
            pltpu.VMEM((8, slots), F32),
            pltpu.VMEM((2, 8, slots), F32),
            pltpu.VMEM((3, planes, slots), F32),
            pltpu.VMEM((3, rows, slots), F32),
            pltpu.VMEM((3, nx, slots), jnp.bfloat16),
            pltpu.VMEM((planes, 4, rows, nx), F32),
            pltpu.VMEM((planes, 4, rows, nx), F32),
            pltpu.VMEM((2, planes, 4, EDGE, nx), F32),
            pltpu.VMEM((4, 2, ny, nx), F32),
            pltpu.VMEM((4, 2, nz, 8, nx), F32),
            pltpu.VMEM((nz + 2, ny, nx), F32),
            pltpu.VMEM((nz + 1, ny, nx), F32),
            own, own, own, own, own,
            own, own, own, own, own,
            pltpu.VMEM((2, 8, 128), F32),
            pltpu.VMEM((2, 8, 128), F32),
            pltpu.VMEM((2, ngy - 1, 8, 128), F32),
            pltpu.VMEM((2, ngz - 1, 8, 128), F32),
            dma((2,)), dma((2,)),
            dma((2, 2)), dma((2, 2)),
            dma((4, 2)), dma((4, 2)), dma((4, 2)), dma((4, 2)),
            dma((2, ngy - 1)), dma((2, ngy - 1)), dma((2, ngz - 1)), dma((2, ngz - 1)), dma((4,)),
        ],
        compiler_params=pltpu.CompilerParams(
            collective_id=0, has_side_effects=True, vmem_limit_bytes=60 * 1024 * 1024
        ),
    )(
        brick_counts, parcel_cell[None, :], parcel_offset, parcel_volume[None, :], parcel_force,
        divergence, pressure_prev, gas_density,
    )
    return pl.pallas_call(
        pass_kernel,
        out_shape=shapes,
        in_specs=[hbm] * 4,
        out_specs=(hbm,) * 4,
        scratch_shapes=bufs + [dma((4, PIECES)), dma((4, PIECES))],
    )(*made)


def solution(mesh):
    ngz, ngy = mesh.shape["gz"], mesh.shape["gy"]
    return jax.shard_map(
        functools.partial(on_device, ngz, ngy),
        mesh=mesh,
        in_specs=(
            P(("gz", "gy")),
            P(None, ("gz", "gy")),
            P(("gz", "gy")),
            P(None, ("gz", "gy")),
            P("gz", "gy"),
            P("gz", "gy", None),
            P("gz", "gy", None),
            P("gz", "gy", None),
        ),
        out_specs=(
            P("gz", "gy", None),
            P("gz", None, "gy", None),
            P("gz", "gy", None),
            P("gz", "gy", None),
        ),
        check_vma=False,
    )
```
